256 devices in a mesh: blk: 8 (over x, y_hi), group: 32 (over z, y_lo, core).
Axes of the slice: x: 4, y: 4 (y_hi: 2, y_lo: 2; y = y_hi * 2 + y_lo), z: 8, core: 2. Of those that a mesh axis runs over, the one named last changes fastest.
Arguments:
- queries: bfloat16 [8, 32, 1024, 768], P('blk', 'group'), may hold values from -12 to 12
- passages: bfloat16 [8, 32, 128, 768], P('blk', 'group'), may hold values from -8 to 8
- hard_negs: bfloat16 [8, 32, 1024, 768], P('blk', 'group'), may hold values from -1.75 to 1.75
- positives: int32 [8, 32, 1024], P('blk', 'group'), may hold values from 0 to 1023
- assign: int32 [32, 32], replicated, may hold values from 0 to 31, each once within a row
Outputs:
- query_loss: float32 [8, 32, 1024], P('blk', 'group')
- query_gradient: float32 [8, 32, 1024, 768], P('blk', 'group')
- grad_passages: float32 [8, 32, 128, 768], P('blk', 'group')
- grad_hard: float32 [8, 32, 1024, 768], P('blk', 'group')
The draws below stay inside these ranges and needn't reach their ends.
Inputs may be any that keep to these rules, and one draw needn't show every extreme that they name: `positives`: row position in the pool of the query's group: the holder's blk index times 128 plus the row. `assign`: each row is a permutation of 0 to 31.
All inputs are finite; a program needn't handle non-finite values.
Results may differ from the reference program's by a relative error of at most 0.0045.
Values may be sent and summed in bfloat16 or wider, within the bound.
No kernel may reach another device: no remote copies, remote signals or barrier semaphores. Data moves between devices by JAX's collectives and lax.ppermute only.
A program may use at most 128 MiB of HBM per device.

```python
import jax
import jax.numpy as jnp
from jax import lax

D = 768
Q_DEV = 1024
P_DEV = 128
H_DEV = 1024
N_BLK = 8
N_GROUP = 32


def embedding_pair(key):
    query_key = jax.random.fold_in(key, 101)
    passage_key = jax.random.fold_in(key, 202)
    query_base = jnp.clip(jax.random.normal(query_key, (N_BLK, N_GROUP, Q_DEV, D), jnp.float32), -4.0, 4.0) * 0.25
    passage_base = jnp.clip(jax.random.normal(passage_key, (N_BLK, N_GROUP, P_DEV, D), jnp.float32), -4.0, 4.0) * 0.3
    query_values = query_base
    passage_values = passage_base
    return (query_values, passage_values)


def draw_queries(key, part):
    query_values, passage_values = embedding_pair(key)
    return query_values.astype(jnp.bfloat16)


def draw_passages(key, part):
    query_values, passage_values = embedding_pair(key)
    return passage_values.astype(jnp.bfloat16)


def with_ends(values, key, smallest, high):
    longest = values.shape.index(max(values.shape))
    spots = []
    for shift in (0, 1):
        where = [jax.random.randint(jax.random.fold_in(key, axis), (), 0, length) for axis, length in enumerate(values.shape)]
        where[longest] = (where[longest] + shift) % values.shape[longest]
        spots.append(tuple(where))
    return values.at[spots[0]].set(smallest).at[spots[1]].set(high)


def steps_of(key, dims, pieces, smallest, top_value):
    gain = 1.0
    for position, shards_of in pieces:
        heights = jax.random.uniform(jax.random.fold_in(jax.random.fold_in(key, 6), position), (shards_of,), jnp.float32, smallest / len(pieces), top_value / len(pieces))
        gain = gain * jnp.repeat(jnp.exp(heights), dims[position] // shards_of).reshape((-1,) + (1,) * (len(dims) - 1 - position))
    return gain


def bell_draw(own_key, dims, deviation, limit, split=(), kind=jnp.bfloat16):
    values = deviation * jax.random.normal(own_key, dims, jnp.float32)
    if split:
        values = values * steps_of(own_key, dims, split, -0.22, 0.18)
    return jnp.clip(values, -limit, limit).astype(kind)


def setup_inputs(seed: int = 0) -> dict:
    arg_keys = jax.random.split(jax.random.key(seed), 6)
    queries = draw_queries(jax.random.fold_in(arg_keys[5], 71), 0)
    passages = draw_passages(jax.random.fold_in(arg_keys[5], 71), 0)
    hard_negs = bell_draw(arg_keys[2], (N_BLK, N_GROUP, H_DEV, D), 0.3, 1.75, ((0, 8), (1, 32)))
    positives = with_ends(jax.random.randint(arg_keys[3], (N_BLK, N_GROUP, Q_DEV), 0, N_BLK * P_DEV), jax.random.fold_in(arg_keys[3], 1), 0, (N_BLK * P_DEV) - 1).astype(jnp.int32)
    assign = jax.vmap(lambda own: jax.random.permutation(own, N_GROUP))(jax.random.split(arg_keys[4], N_GROUP)).reshape((N_GROUP, N_GROUP)).astype(jnp.int32)
    return {"queries": queries, "passages": passages, "hard_negs": hard_negs, "positives": positives, "assign": assign}


def group_terms(query_rows, pool_rows, hard_rows, targets):
    members = query_rows.shape[0]
    pool_all = jnp.broadcast_to(pool_rows[None], (members,) + pool_rows.shape)
    candidate_passages = jnp.concatenate([pool_all, hard_rows], axis=1).astype(jnp.float32)
    query_single_float = query_rows.astype(jnp.float32)
    similarity_scores = jnp.einsum("zno,zso->zns", query_single_float, candidate_passages, precision=lax.Precision.HIGHEST)
    highest = jnp.max(similarity_scores, axis=2, keepdims=True)
    log_total = highest + jnp.log(jnp.sum(jnp.exp(similarity_scores - highest), axis=2, keepdims=True))
    column_ids = jnp.arange(similarity_scores.shape[2], dtype=jnp.int32)
    one_hot = (column_ids[None, None, :] == targets[:, :, None]).astype(jnp.float32)
    picked = jnp.sum(similarity_scores * one_hot, axis=2)
    query_loss = log_total[:, :, 0] - picked
    weights = (jnp.exp(similarity_scores - log_total) - one_hot).astype(jnp.bfloat16)
    weight_single_float = weights.astype(jnp.float32)
    query_gradient = jnp.einsum("kau,kuj->kaj", weight_single_float, candidate_passages, precision=lax.Precision.HIGHEST)
    pool_column_count = pool_rows.shape[0]
    pool_gradient = jnp.einsum("kgx,kgo->xo", weight_single_float[:, :, :pool_column_count], query_single_float, precision=lax.Precision.HIGHEST)
    gradient_group_set = jnp.einsum("vka,vke->vae", weight_single_float[:, :, pool_column_count:], query_single_float, precision=lax.Precision.HIGHEST)
    return query_loss, query_gradient, pool_gradient, gradient_group_set


def reference(queries, passages, hard_negs, positives, assign):
    members = queries.shape[0]
    groups = queries.shape[1]
    block_rows = passages.shape[2]
    feature_width = queries.shape[3]
    slice_rows = hard_negs.shape[2] // groups
    slot_ids = jnp.arange(groups, dtype=jnp.int32)
    inverse = jnp.sum(slot_ids[None, None, :] * (assign[:, None, :] == slot_ids[None, :, None]).astype(jnp.int32), axis=2)
    hard_split = hard_negs.reshape(members, groups, groups, slice_rows, feature_width)

    def per_group(group_index):
        query_rows = queries[:, group_index]
        pool_rows = passages[:, group_index].reshape(members * block_rows, feature_width)
        chosen = hard_split[:, slot_ids, inverse[:, group_index]]
        hard_rows = chosen.reshape(members, groups * slice_rows, feature_width)
        return group_terms(query_rows, pool_rows, hard_rows, positives[:, group_index])

    query_loss, query_gradient, pool_gradient, gradient_group_set = lax.map(per_group, slot_ids)
    query_loss = jnp.transpose(query_loss, (1, 0, 2))
    query_gradient = jnp.transpose(query_gradient, (1, 0, 2, 3))
    grad_passages = jnp.transpose(pool_gradient.reshape(groups, members, block_rows, feature_width), (1, 0, 2, 3))
    grad_split = gradient_group_set.reshape(groups, members, groups, slice_rows, feature_width)
    placed = grad_split[assign, :, slot_ids[:, None]]
    grad_hard = jnp.transpose(placed, (2, 0, 1, 3, 4)).reshape(members, groups, groups * slice_rows, feature_width)
    return query_loss, query_gradient, grad_passages, grad_hard
```

```python
import functools

import jax
import jax.numpy as jnp
from jax import lax
from jax.experimental import pallas as pl
from jax.experimental.pallas import tpu as pltpu
from jax.sharding import PartitionSpec as P


def shifted(array, axis, by):
    count = lax.axis_size(axis)
    return lax.ppermute(array, axis, [(i, (i + by) % count) for i in range(count)])


def cross_rows(left_rows, right_rows):
    return lax.dot_general(
        left_rows, right_rows, (((1,), (1,)), ((), ())), preferred_element_type=jnp.float32
    )


def column_terms(weights, query_rows):
    return lax.dot_general(
        weights, query_rows, (((0,), (0,)), ((), ())), preferred_element_type=jnp.float32
    )


def place_slices_kernel(groups, slice_rows, row_ref, hard_ref, out_ref, sem):
    copies = []
    for k in range(groups):
        target = pl.multiple_of(row_ref[k] * slice_rows, slice_rows)
        copy = pltpu.make_async_copy(
            hard_ref.at[pl.ds(k * slice_rows, slice_rows)],
            out_ref.at[pl.ds(target, slice_rows)],
            sem.at[k],
        )
        copy.start()
        copies.append(copy)
    for copy in copies:
        copy.wait()


def place_slices(assign_row, hard_rows, groups):
    rows, width = hard_rows.shape
    return pl.pallas_call(
        functools.partial(place_slices_kernel, groups, rows // groups),
        out_shape=jax.ShapeDtypeStruct(hard_rows.shape, hard_rows.dtype),
        grid_spec=pltpu.PrefetchScalarGridSpec(
            num_scalar_prefetch=1,
            grid=(1,),
            in_specs=[pl.BlockSpec(memory_space=pl.ANY)],
            out_specs=pl.BlockSpec((rows, width), lambda i, row: (0, 0)),
            scratch_shapes=[pltpu.SemaphoreType.DMA((groups,))],
        ),
        name="place_slices",
    )(assign_row, hard_rows)


def fetch_slices_kernel(per_step, slice_rows, row_ref, back_ref, out_ref):
    step = pl.program_id(0)
    for j in range(per_step):
        source = pl.multiple_of(row_ref[step * per_step + j] * slice_rows, slice_rows)
        out_ref[pl.ds(j * slice_rows, slice_rows), :] = back_ref[
            pl.ds(source, slice_rows), :
        ].astype(jnp.float32)


def fetch_slices(assign_row, returned, groups):
    rows, width = returned.shape
    steps = 8
    per_step, slice_rows = groups // steps, rows // groups
    return pl.pallas_call(
        functools.partial(fetch_slices_kernel, per_step, slice_rows),
        out_shape=jax.ShapeDtypeStruct(returned.shape, jnp.float32),
        grid_spec=pltpu.PrefetchScalarGridSpec(
            num_scalar_prefetch=1,
            grid=(steps,),
            in_specs=[pl.BlockSpec((rows, width), lambda i, row: (0, 0))],
            out_specs=pl.BlockSpec((per_step * slice_rows, width), lambda i, row: (i, 0)),
        ),
        name="fetch_slices",
    )(assign_row, returned)


def per_device(queries, passages, hard_negs, positives, assign):
    query_rows = queries[0, 0]
    own_block = passages[0, 0]
    hard_rows = hard_negs[0, 0]
    targets = positives[0, 0]
    members = lax.axis_size("blk")
    groups = lax.axis_size("group")
    member_index = lax.axis_index("blk")
    group_index = lax.axis_index("group")
    block_rows = own_block.shape[0]
    pool_column_count = members * block_rows
    assign_row = lax.dynamic_index_in_dim(assign, group_index, 0, keepdims=False)

    outgoing = place_slices(assign_row, hard_rows, groups)
    hard_set = lax.all_to_all(outgoing, "group", split_axis=0, concat_axis=0, tiled=True)

    arrived = [own_block] + [shifted(own_block, "blk", by) for by in range(1, members)]
    pool_matrix = jnp.concatenate(arrived, axis=0)
    pool_scores = cross_rows(query_rows, pool_matrix)
    source_blk = targets // block_rows
    offsets = (member_index - source_blk) % members
    pool_columns = offsets * block_rows + targets % block_rows
    column_ids = jnp.arange(pool_column_count, dtype=jnp.int32)
    one_hot = (column_ids[None, :] == pool_columns[:, None]).astype(jnp.float32)
    picked = jnp.sum(pool_scores * one_hot, axis=1)
    pool_highest = jnp.max(pool_scores, axis=1, keepdims=True)
    pool_sum = jnp.sum(jnp.exp(pool_scores - pool_highest), axis=1, keepdims=True)

    hard_scores = cross_rows(query_rows, hard_set)
    highest = jnp.maximum(pool_highest, jnp.max(hard_scores, axis=1, keepdims=True))
    summed_exp = pool_sum * jnp.exp(pool_highest - highest) + jnp.sum(
        jnp.exp(hard_scores - highest), axis=1, keepdims=True
    )
    log_total = highest + jnp.log(summed_exp)
    query_loss = log_total[:, 0] - picked
    hard_weights = jnp.exp(hard_scores - log_total).astype(jnp.bfloat16)
    hard_terms = column_terms(hard_weights, query_rows).astype(jnp.bfloat16)
    returned = lax.all_to_all(hard_terms, "group", split_axis=0, concat_axis=0, tiled=True)

    pool_weights = (jnp.exp(pool_scores - log_total) - one_hot).astype(jnp.bfloat16)
    pool_terms = column_terms(pool_weights, query_rows)
    sent_terms = pool_terms.astype(jnp.bfloat16)
    grad_passages = pool_terms[:block_rows]
    for by in range(1, members):
        part = lax.slice_in_dim(sent_terms, by * block_rows, (by + 1) * block_rows, axis=0)
        grad_passages = grad_passages + shifted(part, "blk", -by).astype(jnp.float32)
    query_gradient = jnp.dot(pool_weights, pool_matrix, preferred_element_type=jnp.float32)
    query_gradient = query_gradient + jnp.dot(
        hard_weights, hard_set, preferred_element_type=jnp.float32
    )
    grad_hard = fetch_slices(assign_row, returned, groups)
    return (
        query_loss[None, None],
        query_gradient[None, None],
        grad_passages[None, None],
        grad_hard[None, None],
    )


def solution(mesh):
    placed = (
        P("blk", "group", None, None),
        P("blk", "group", None, None),
        P("blk", "group", None, None),
        P("blk", "group", None),
        P(),
    )
    return jax.shard_map(
        per_device,
        mesh=mesh,
        in_specs=placed,
        out_specs=(
            P("blk", "group", None),
            P("blk", "group", None, None),
            P("blk", "group", None, None),
            P("blk", "group", None, None),
        ),
        check_vma=False,
    )
```

```python
import functools

import jax
import jax.numpy as jnp
from jax import lax
from jax.experimental import pallas as pl
from jax.experimental.pallas import tpu as pltpu
from jax.sharding import PartitionSpec as P

VMEM = pl.BlockSpec(memory_space=pltpu.VMEM)
HBM = pl.BlockSpec(memory_space=pltpu.HBM)
MIB = 1 << 20


def in_hbm(array):
    return pltpu.with_memory_space_constraint(array, pltpu.HBM)


def moved(array, dx, dy):
    count = lax.axis_size("blk")
    pairs = [(i, ((i // 2 + dx) % (count // 2)) * 2 + ((i % 2) ^ dy)) for i in range(count)]
    return lax.ppermute(array, "blk", pairs)


def dot_rows(left, right):
    return lax.dot_general(
        left, right, (((1,), (1,)), ((), ())), preferred_element_type=jnp.float32
    )


def dot_plain(left, right):
    return lax.dot_general(
        left, right, (((1,), (0,)), ((), ())), preferred_element_type=jnp.float32
    )


def dot_columns(left, right):
    return lax.dot_general(
        left, right, (((0,), (0,)), ((), ())), preferred_element_type=jnp.float32
    )


def place_slices_kernel(groups, slice_rows, assign_ref, hard_ref, out_ref, row, held, sem_row, sem_in, sem_out):
    own = lax.axis_index("group")
    load = pltpu.make_async_copy(assign_ref.at[own], row, sem_row)
    load.start()
    gets, puts = [], []
    for k in range(groups):
        here = pl.ds(k * slice_rows, slice_rows)
        gets.append(pltpu.make_async_copy(hard_ref.at[here], held.at[here], sem_in.at[k]))
        gets[-1].start()
    load.wait()
    for k in range(groups):
        here = pl.ds(k * slice_rows, slice_rows)
        there = pl.ds(pl.multiple_of(row[k] * slice_rows, slice_rows), slice_rows)
        gets[k].wait()
        puts.append(pltpu.make_async_copy(held.at[here], out_ref.at[there], sem_out.at[k]))
        puts[-1].start()
    for put in puts:
        put.wait()


def place_slices(assign, hard_rows, groups):
    return pl.pallas_call(
        functools.partial(place_slices_kernel, groups, hard_rows.shape[0] // groups),
        out_shape=pltpu.HBM(hard_rows.shape, hard_rows.dtype),
        in_specs=[HBM, HBM],
        out_specs=HBM,
        scratch_shapes=[
            pltpu.SMEM((groups,), jnp.int32),
            pltpu.VMEM(hard_rows.shape, hard_rows.dtype),
            pltpu.SemaphoreType.DMA,
            pltpu.SemaphoreType.DMA((groups,)),
            pltpu.SemaphoreType.DMA((groups,)),
        ],
        compiler_params=pltpu.CompilerParams(vmem_limit_bytes=4 * MIB),
        name="place_slices",
    )(in_hbm(assign), in_hbm(hard_rows))


def fetch_slices_kernel(groups, slice_rows, assign_ref, back_ref, out_ref, row, held, sem_row, sem):
    own = lax.axis_index("group")
    load = pltpu.make_async_copy(assign_ref.at[own], row, sem_row)
    load.start()
    load.wait()
    puts = []
    for k in range(groups):
        here = pl.ds(k * slice_rows, slice_rows)
        there = pl.ds(pl.multiple_of(row[k] * slice_rows, slice_rows), slice_rows)
        held[here, :] = back_ref[there, :].astype(jnp.float32)
        puts.append(pltpu.make_async_copy(held.at[here], out_ref.at[here], sem.at[k]))
        puts[-1].start()
    for put in puts:
        put.wait()


def fetch_slices(assign, returned, groups):
    return pl.pallas_call(
        functools.partial(fetch_slices_kernel, groups, returned.shape[0] // groups),
        out_shape=pltpu.HBM(returned.shape, jnp.float32),
        in_specs=[HBM, VMEM],
        out_specs=HBM,
        scratch_shapes=[
            pltpu.SMEM((groups,), jnp.int32),
            pltpu.VMEM(returned.shape, jnp.float32),
            pltpu.SemaphoreType.DMA,
            pltpu.SemaphoreType.DMA((groups,)),
        ],
        compiler_params=pltpu.CompilerParams(vmem_limit_bytes=6 * MIB),
        name="fetch_slices",
    )(in_hbm(assign), returned)


def pool_kernel(part, column_ref, query_ref, *refs):
    block_refs, (pool_out, score_out, stat_out, pool, score, stat, sem) = refs[:-7], refs[-7:]
    rows = block_refs[0].shape[0]
    for c, block in enumerate(block_refs):
        pool[pl.ds(c * rows, rows), :] = block[...]
    puts = [pltpu.make_async_copy(pool, pool_out, sem.at[0])]
    puts[0].start()
    columns = column_ref[...]
    highest, picked = None, None
    steps = range(0, pool.shape[0], part)
    for n, start in enumerate(steps):
        here = pl.ds(start, part)
        scores = dot_rows(pool[here, :], query_ref[...])
        score[here, :] = scores
        puts.append(pltpu.make_async_copy(score.at[here], score_out.at[here], sem.at[n + 2]))
        puts[-1].start()
        ids = start + lax.broadcasted_iota(jnp.int32, scores.shape, 0)
        peak = jnp.max(scores, axis=0, keepdims=True)
        hit = jnp.sum(jnp.where(ids == columns, scores, 0.0), axis=0, keepdims=True)
        highest = peak if highest is None else jnp.maximum(highest, peak)
        picked = hit if picked is None else picked + hit
    total = None
    for start in steps:
        some = jnp.sum(jnp.exp(score[pl.ds(start, part), :] - highest), axis=0, keepdims=True)
        total = some if total is None else total + some
    stat[0:1, :] = highest
    stat[1:2, :] = total
    stat[2:3, :] = picked
    stat[3:8, :] = jnp.zeros_like(stat[3:8, :])
    puts.append(pltpu.make_async_copy(stat, stat_out, sem.at[1]))
    puts[-1].start()
    for put in puts:
        put.wait()


def pool_stage(columns, query_rows, blocks):
    rows, width = len(blocks) * blocks[0].shape[0], query_rows.shape[1]
    queries = query_rows.shape[0]
    part = 256
    return pl.pallas_call(
        functools.partial(pool_kernel, part),
        out_shape=(
            pltpu.HBM((rows, width), query_rows.dtype),
            pltpu.HBM((rows, queries), jnp.float32),
            pltpu.HBM((8, queries), jnp.float32),
        ),
        in_specs=[VMEM] * (2 + len(blocks)),
        out_specs=(HBM, HBM, HBM),
        scratch_shapes=[
            pltpu.VMEM((rows, width), query_rows.dtype),
            pltpu.VMEM((rows, queries), jnp.float32),
            pltpu.VMEM((8, queries), jnp.float32),
            pltpu.SemaphoreType.DMA((2 + rows // part,)),
        ],
        compiler_params=pltpu.CompilerParams(vmem_limit_bytes=16 * MIB),
        cost_estimate=pl.CostEstimate(
            flops=2 * rows * queries * width, bytes_accessed=8 * MIB, transcendentals=rows * queries
        ),
        name="pool_stage",
    )(columns, query_rows, *blocks)


def hard_kernel(
    part, chunk, hard_ref, query_ref, stat_ref, term_ref, weight_out, lse_ref, loss_ref, stat, score, weight, held, sem
):
    queries, rows = query_ref.shape[0], hard_ref.shape[0]
    load = pltpu.make_async_copy(stat_ref, stat, sem.at[0])
    load.start()
    steps = range(0, queries, part)

    def scores_of(start):
        score[:, pl.ds(start, part)] = dot_rows(hard_ref[...], query_ref[pl.ds(start, part), :])

    scores_of(0)
    load.wait()
    for start in steps:
        if start + part < queries:
            scores_of(start + part)
        here = pl.ds(start, part)
        pool_highest = stat[0:1, here]
        highest = jnp.maximum(pool_highest, jnp.max(score[:, here], axis=0, keepdims=True))
        raised = jnp.exp(score[:, here] - highest)
        total = stat[1:2, here] * jnp.exp(pool_highest - highest) + jnp.sum(
            raised, axis=0, keepdims=True
        )
        weight[:, here] = (raised * (1.0 / total)).astype(weight.dtype)
        lse = highest + jnp.log(total)
        lse_ref[:, here] = lse
        loss_ref[:, here] = lse - stat[2:3, here]
    puts = [pltpu.make_async_copy(weight, weight_out, sem.at[1])]
    for n, start in enumerate(range(0, rows, chunk)):
        here = pl.ds(start, chunk)
        held[here, :] = dot_plain(weight[here, :], query_ref[...]).astype(held.dtype)
        puts.append(pltpu.make_async_copy(held.at[here], term_ref.at[here], sem.at[n + 2]))
        puts[-1].start()
        if n == 0:
            puts[0].start()
    for put in puts:
        put.wait()


def hard_stage(hard_set, query_rows, stats):
    rows, width = hard_set.shape
    queries = query_rows.shape[0]
    part, chunk = 256, 256
    return pl.pallas_call(
        functools.partial(hard_kernel, part, chunk),
        out_shape=(
            pltpu.HBM((rows, width), jnp.bfloat16),
            pltpu.HBM((rows, queries), jnp.bfloat16),
            jax.ShapeDtypeStruct((1, queries), jnp.float32),
            jax.ShapeDtypeStruct((1, queries), jnp.float32),
        ),
        in_specs=[VMEM, VMEM, HBM],
        out_specs=(HBM, HBM, VMEM, VMEM),
        scratch_shapes=[
            pltpu.VMEM(stats.shape, jnp.float32),
            pltpu.VMEM((rows, queries), jnp.float32),
            pltpu.VMEM((rows, queries), jnp.bfloat16),
            pltpu.VMEM((rows, width), jnp.bfloat16),
            pltpu.SemaphoreType.DMA((2 + rows // chunk,)),
        ],
        compiler_params=pltpu.CompilerParams(vmem_limit_bytes=20 * MIB),
        cost_estimate=pl.CostEstimate(
            flops=4 * rows * queries * width, bytes_accessed=8 * MIB, transcendentals=rows * queries
        ),
        name="hard_stage",
    )(hard_set, query_rows, in_hbm(stats))


def pool_back_kernel(part, score_ref, column_ref, query_ref, lse_ref, weight_ref, near_ref, *block_refs):
    rows = near_ref.shape[0]
    columns, lse = column_ref[...], lse_ref[...]
    for start in range(0, score_ref.shape[0], part):
        here = pl.ds(start, part)
        ids = start + lax.broadcasted_iota(jnp.int32, (part, columns.shape[1]), 0)
        chance = jnp.exp(score_ref[here, :] - lse)
        weight_ref[here, :] = jnp.where(ids == columns, chance - 1.0, chance).astype(weight_ref.dtype)
        terms = dot_plain(weight_ref[here, :], query_ref[...])
        for j in range(part // rows):
            piece = terms[j * rows : (j + 1) * rows]
            n = start // rows + j
            if n == 0:
                near_ref[...] = piece
            else:
                block_refs[n - 1][...] = piece.astype(block_refs[n - 1].dtype)


def pool_back_stage(scores, columns, query_rows, lse, block_rows):
    rows, queries = scores.shape
    width = query_rows.shape[1]
    others = rows // block_rows - 1
    return pl.pallas_call(
        functools.partial(pool_back_kernel, 256),
        out_shape=(
            jax.ShapeDtypeStruct((rows, queries), jnp.bfloat16),
            jax.ShapeDtypeStruct((block_rows, width), jnp.float32),
        )
        + (jax.ShapeDtypeStruct((block_rows, width), jnp.bfloat16),) * others,
        in_specs=[VMEM] * 4,
        out_specs=(VMEM,) * (2 + others),
        compiler_params=pltpu.CompilerParams(vmem_limit_bytes=24 * MIB),
        cost_estimate=pl.CostEstimate(
            flops=2 * rows * queries * width, bytes_accessed=8 * MIB, transcendentals=rows * queries
        ),
        name="pool_back_stage",
    )(scores, columns, query_rows, lse)


def per_device(queries, passages, hard_negs, positives, assign):
    query_rows = queries[0, 0]
    own_block = passages[0, 0]
    hard_rows = hard_negs[0, 0]
    targets = positives[0]
    across = lax.axis_size("blk") // 2
    groups = lax.axis_size("group")
    member_index = lax.axis_index("blk")
    block_rows = own_block.shape[0]

    outgoing = place_slices(assign, hard_rows, groups)
    hard_set = lax.all_to_all(outgoing, "group", split_axis=0, concat_axis=0, tiled=True)

    steps_x = [2, 1, 3] if across == 4 else list(range(1, across))
    other_block = moved(own_block, 0, 1)
    blocks = [own_block, other_block] + [None] * (2 * across - 2)
    for dx in steps_x:
        blocks[2 * dx] = moved(own_block, dx, 0)
    for dx in steps_x:
        blocks[2 * dx + 1] = moved(other_block, dx, 0)
    source = targets // block_rows
    back = (member_index // 2 - source // 2) % across
    flip = (member_index + source) % 2
    columns = (back * 2 + flip) * block_rows + targets % block_rows
    pool_matrix, pool_scores, stats = pool_stage(columns, query_rows, blocks)

    hard_terms, hard_weights, lse, loss = hard_stage(hard_set, query_rows, stats)
    returned = lax.all_to_all(hard_terms, "group", split_axis=0, concat_axis=0, tiled=True)

    pool_weights, near, *terms = pool_back_stage(pool_scores, columns, query_rows, lse, block_rows)
    terms = [None] + terms
    far = terms[1].astype(jnp.float32)
    arrivals = [moved(terms[2 * dx + 1], -dx, 0) for dx in steps_x]
    for arrival in arrivals:
        far = far + arrival.astype(jnp.float32)
    arrivals = [moved(terms[2 * dx], -dx, 0) for dx in steps_x]
    arrivals.append(moved(far.astype(jnp.bfloat16), 0, 1))
    grad_passages = near
    for arrival in arrivals:
        grad_passages = grad_passages + arrival.astype(jnp.float32)
    query_gradient = dot_columns(pool_weights, pool_matrix) + dot_columns(hard_weights, hard_set)
    grad_hard = fetch_slices(assign, returned, groups)
    return (
        loss[None],
        query_gradient[None, None],
        grad_passages[None, None],
        grad_hard[None, None],
    )


def solution(mesh):
    placed = (
        P("blk", "group", None, None),
        P("blk", "group", None, None),
        P("blk", "group", None, None),
        P("blk", "group", None),
        P(),
    )
    return jax.shard_map(
        per_device,
        mesh=mesh,
        in_specs=placed,
        out_specs=(
            P("blk", "group", None),
            P("blk", "group", None, None),
            P("blk", "group", None, None),
            P("blk", "group", None, None),
        ),
        check_vma=False,
    )
```

```python
import functools

import jax
import jax.numpy as jnp
from jax import lax
from jax.experimental import pallas as pl
from jax.experimental.pallas import tpu as pltpu
from jax.sharding import PartitionSpec as P

VMEM = pl.BlockSpec(memory_space=pltpu.VMEM)
HBM = pl.BlockSpec(memory_space=pltpu.HBM)
MIB = 1 << 20


def in_hbm(array):
    return pltpu.with_memory_space_constraint(array, pltpu.HBM)


def moved(array, dx, dy):
    count = lax.axis_size("blk")
    pairs = [(i, ((i // 2 + dx) % (count // 2)) * 2 + ((i % 2) ^ dy)) for i in range(count)]
    return lax.ppermute(array, "blk", pairs)


def dot_rows(left, right):
    return lax.dot_general(
        left, right, (((1,), (1,)), ((), ())), preferred_element_type=jnp.float32
    )


def dot_plain(left, right):
    return lax.dot_general(
        left, right, (((1,), (0,)), ((), ())), preferred_element_type=jnp.float32
    )


def dot_columns(left, right):
    return lax.dot_general(
        left, right, (((0,), (0,)), ((), ())), preferred_element_type=jnp.float32
    )


def place_slices_kernel(groups, slice_rows, assign_ref, hard_ref, out_ref, row, held, sem_row, sem_in, sem_out):
    own = lax.axis_index("group")
    load = pltpu.make_async_copy(assign_ref.at[own], row, sem_row)
    load.start()
    gets, puts = [], []
    for k in range(groups):
        here = pl.ds(k * slice_rows, slice_rows)
        gets.append(pltpu.make_async_copy(hard_ref.at[here], held.at[here], sem_in.at[k]))
        gets[-1].start()
    load.wait()
    for k in range(groups):
        here = pl.ds(k * slice_rows, slice_rows)
        there = pl.ds(pl.multiple_of(row[k] * slice_rows, slice_rows), slice_rows)
        gets[k].wait()
        puts.append(pltpu.make_async_copy(held.at[here], out_ref.at[there], sem_out.at[k]))
        puts[-1].start()
    for put in puts:
        put.wait()


def place_slices(assign, hard_rows, groups):
    return pl.pallas_call(
        functools.partial(place_slices_kernel, groups, hard_rows.shape[0] // groups),
        out_shape=pltpu.HBM(hard_rows.shape, hard_rows.dtype),
        in_specs=[HBM, HBM],
        out_specs=HBM,
        scratch_shapes=[
            pltpu.SMEM((groups,), jnp.int32),
            pltpu.VMEM(hard_rows.shape, hard_rows.dtype),
            pltpu.SemaphoreType.DMA,
            pltpu.SemaphoreType.DMA((groups,)),
            pltpu.SemaphoreType.DMA((groups,)),
        ],
        compiler_params=pltpu.CompilerParams(vmem_limit_bytes=4 * MIB),
        name="place_slices",
    )(in_hbm(assign), in_hbm(hard_rows))


def fetch_slices_kernel(groups, slice_rows, assign_ref, back_ref, out_ref, row, held, sem_row, sem):
    own = lax.axis_index("group")
    load = pltpu.make_async_copy(assign_ref.at[own], row, sem_row)
    load.start()
    held[...] = back_ref[...].astype(jnp.float32)
    load.wait()
    puts = []
    for k in range(groups):
        here = pl.ds(k * slice_rows, slice_rows)
        there = pl.ds(pl.multiple_of(row[k] * slice_rows, slice_rows), slice_rows)
        puts.append(pltpu.make_async_copy(held.at[there], out_ref.at[here], sem.at[k]))
        puts[-1].start()
    for put in puts:
        put.wait()


def fetch_slices(assign, returned, groups):
    return pl.pallas_call(
        functools.partial(fetch_slices_kernel, groups, returned.shape[0] // groups),
        out_shape=pltpu.HBM(returned.shape, jnp.float32),
        in_specs=[HBM, VMEM],
        out_specs=HBM,
        scratch_shapes=[
            pltpu.SMEM((groups,), jnp.int32),
            pltpu.VMEM(returned.shape, jnp.float32),
            pltpu.SemaphoreType.DMA,
            pltpu.SemaphoreType.DMA((groups,)),
        ],
        compiler_params=pltpu.CompilerParams(vmem_limit_bytes=6 * MIB),
        name="fetch_slices",
    )(in_hbm(assign), returned)


def pool_kernel(part, column_ref, query_ref, *refs):
    block_refs, (pool_out, stat_out, pool, score, stat, sem) = refs[:-6], refs[-6:]
    rows = block_refs[0].shape[0]
    for c, block in enumerate(block_refs):
        pool[pl.ds(c * rows, rows), :] = block[...]
    put_pool = pltpu.make_async_copy(pool, pool_out, sem.at[0])
    put_pool.start()
    columns = column_ref[...]
    highest, picked = None, None
    steps = range(0, pool.shape[0], part)
    for start in steps:
        here = pl.ds(start, part)
        scores = dot_rows(pool[here, :], query_ref[...])
        score[here, :] = scores
        ids = start + lax.broadcasted_iota(jnp.int32, scores.shape, 0)
        peak = jnp.max(scores, axis=0, keepdims=True)
        hit = jnp.sum(jnp.where(ids == columns, scores, 0.0), axis=0, keepdims=True)
        highest = peak if highest is None else jnp.maximum(highest, peak)
        picked = hit if picked is None else picked + hit
    total = None
    for start in steps:
        some = jnp.sum(jnp.exp(score[pl.ds(start, part), :] - highest), axis=0, keepdims=True)
        total = some if total is None else total + some
    stat[0:1, :] = highest
    stat[1:2, :] = total
    stat[2:3, :] = picked
    stat[3:8, :] = jnp.zeros_like(stat[3:8, :])
    put_stat = pltpu.make_async_copy(stat, stat_out, sem.at[1])
    put_stat.start()
    put_pool.wait()
    put_stat.wait()


def pool_stage(columns, query_rows, blocks):
    rows, width = len(blocks) * blocks[0].shape[0], query_rows.shape[1]
    queries = query_rows.shape[0]
    return pl.pallas_call(
        functools.partial(pool_kernel, 512),
        out_shape=(
            pltpu.HBM((rows, width), query_rows.dtype),
            pltpu.HBM((8, queries), jnp.float32),
        ),
        in_specs=[VMEM] * (2 + len(blocks)),
        out_specs=(HBM, HBM),
        scratch_shapes=[
            pltpu.VMEM((rows, width), query_rows.dtype),
            pltpu.VMEM((rows, queries), jnp.float32),
            pltpu.VMEM((8, queries), jnp.float32),
            pltpu.SemaphoreType.DMA((2,)),
        ],
        compiler_params=pltpu.CompilerParams(vmem_limit_bytes=16 * MIB),
        cost_estimate=pl.CostEstimate(
            flops=2 * rows * queries * width, bytes_accessed=4 * MIB, transcendentals=rows * queries
        ),
        name="pool_stage",
    )(columns, query_rows, *blocks)


def hard_kernel(
    part, chunks, hard_ref, query_ref, stat_ref, term_ref, lse_ref, loss_ref, stat, score, weight, held, sem
):
    queries = query_ref.shape[0]
    load = pltpu.make_async_copy(stat_ref, stat, sem.at[0])
    load.start()
    steps = range(0, queries, part)

    def scores_of(start):
        score[:, pl.ds(start, part)] = dot_rows(hard_ref[...], query_ref[pl.ds(start, part), :])

    scores_of(0)
    load.wait()
    for start in steps:
        if start + part < queries:
            scores_of(start + part)
        here = pl.ds(start, part)
        pool_highest = stat[0:1, here]
        highest = jnp.maximum(pool_highest, jnp.max(score[:, here], axis=0, keepdims=True))
        raised = jnp.exp(score[:, here] - highest)
        total = stat[1:2, here] * jnp.exp(pool_highest - highest) + jnp.sum(
            raised, axis=0, keepdims=True
        )
        weight[:, here] = (raised * (1.0 / total)).astype(weight.dtype)
        lse = highest + jnp.log(total)
        lse_ref[:, here] = lse
        loss_ref[:, here] = lse - stat[2:3, here]
    puts, start = [], 0
    for n, chunk in enumerate(chunks):
        here = pl.ds(start, chunk)
        held[here, :] = dot_plain(weight[here, :], query_ref[...]).astype(held.dtype)
        puts.append(pltpu.make_async_copy(held.at[here], term_ref.at[here], sem.at[n + 1]))
        puts[-1].start()
        start += chunk
    for put in puts:
        put.wait()


def hard_stage(hard_set, query_rows, stats):
    rows, width = hard_set.shape
    queries = query_rows.shape[0]
    chunks = (rows // 2, rows // 4, rows // 4)
    return pl.pallas_call(
        functools.partial(hard_kernel, queries // 2, chunks),
        out_shape=(
            pltpu.HBM((rows, width), jnp.bfloat16),
            jax.ShapeDtypeStruct((1, queries), jnp.float32),
            jax.ShapeDtypeStruct((1, queries), jnp.float32),
        ),
        in_specs=[VMEM, VMEM, HBM],
        out_specs=(HBM, VMEM, VMEM),
        scratch_shapes=[
            pltpu.VMEM(stats.shape, jnp.float32),
            pltpu.VMEM((rows, queries), jnp.float32),
            pltpu.VMEM((rows, queries), jnp.bfloat16),
            pltpu.VMEM((rows, width), jnp.bfloat16),
            pltpu.SemaphoreType.DMA((1 + len(chunks),)),
        ],
        compiler_params=pltpu.CompilerParams(vmem_limit_bytes=20 * MIB),
        cost_estimate=pl.CostEstimate(
            flops=4 * rows * queries * width, bytes_accessed=8 * MIB, transcendentals=rows * queries
        ),
        name="hard_stage",
    )(hard_set, query_rows, in_hbm(stats))


def query_kernel(part, hard_ref, pool_ref, query_ref, lse_ref, pool_weight_ref, out_ref, weight, held, sem):
    queries = query_ref.shape[0]
    puts = []
    for n, start in enumerate(range(0, queries, part)):
        here = pl.ds(start, part)
        scores = dot_rows(hard_ref[...], query_ref[here, :])
        weight[:, here] = jnp.exp(scores - lse_ref[:, here]).astype(weight.dtype)
        held[here, :] = dot_columns(weight[:, here], hard_ref[...]) + dot_columns(
            pool_weight_ref[:, here], pool_ref[...]
        )
        puts.append(pltpu.make_async_copy(held.at[here], out_ref.at[here], sem.at[n]))
        puts[-1].start()
    for put in puts:
        put.wait()


def query_stage(hard_set, pool_matrix, query_rows, lse, pool_weights):
    queries, width = query_rows.shape
    rows = hard_set.shape[0]
    part = 256
    return pl.pallas_call(
        functools.partial(query_kernel, part),
        out_shape=pltpu.HBM((queries, width), jnp.float32),
        in_specs=[VMEM] * 5,
        out_specs=HBM,
        scratch_shapes=[
            pltpu.VMEM((rows, queries), jnp.bfloat16),
            pltpu.VMEM((queries, width), jnp.float32),
            pltpu.SemaphoreType.DMA((queries // part,)),
        ],
        compiler_params=pltpu.CompilerParams(vmem_limit_bytes=24 * MIB),
        cost_estimate=pl.CostEstimate(
            flops=6 * rows * queries * width, bytes_accessed=8 * MIB, transcendentals=rows * queries
        ),
        name="query_stage",
    )(hard_set, pool_matrix, query_rows, lse, pool_weights)


def pool_back_kernel(part, pool_ref, column_ref, query_ref, lse_ref, weight_ref, near_ref, *block_refs):
    rows = near_ref.shape[0]
    columns, lse = column_ref[...], lse_ref[...]
    for start in range(0, pool_ref.shape[0], part):
        here = pl.ds(start, part)
        ids = start + lax.broadcasted_iota(jnp.int32, (part, columns.shape[1]), 0)
        chance = jnp.exp(dot_rows(pool_ref[here, :], query_ref[...]) - lse)
        weight_ref[here, :] = jnp.where(ids == columns, chance - 1.0, chance).astype(weight_ref.dtype)
        terms = dot_plain(weight_ref[here, :], query_ref[...])
        for j in range(part // rows):
            piece = terms[j * rows : (j + 1) * rows]
            n = start // rows + j
            if n == 0:
                near_ref[...] = piece
            else:
                block_refs[n - 1][...] = piece.astype(block_refs[n - 1].dtype)


def pool_back_stage(pool_matrix, columns, query_rows, lse, block_rows):
    rows, width = pool_matrix.shape
    queries = query_rows.shape[0]
    others = rows // block_rows - 1
    return pl.pallas_call(
        functools.partial(pool_back_kernel, 256),
        out_shape=(
            jax.ShapeDtypeStruct((rows, queries), jnp.bfloat16),
            jax.ShapeDtypeStruct((block_rows, width), jnp.float32),
        )
        + (jax.ShapeDtypeStruct((block_rows, width), jnp.bfloat16),) * others,
        in_specs=[VMEM] * 4,
        out_specs=(VMEM,) * (2 + others),
        compiler_params=pltpu.CompilerParams(vmem_limit_bytes=24 * MIB),
        cost_estimate=pl.CostEstimate(
            flops=4 * rows * queries * width, bytes_accessed=8 * MIB, transcendentals=rows * queries
        ),
        name="pool_back_stage",
    )(pool_matrix, columns, query_rows, lse)


def per_device(queries, passages, hard_negs, positives, assign):
    query_rows = queries[0, 0]
    own_block = passages[0, 0]
    hard_rows = hard_negs[0, 0]
    targets = positives[0]
    across = lax.axis_size("blk") // 2
    groups = lax.axis_size("group")
    member_index = lax.axis_index("blk")
    block_rows = own_block.shape[0]

    outgoing = place_slices(assign, hard_rows, groups)
    hard_set = lax.all_to_all(outgoing, "group", split_axis=0, concat_axis=0, tiled=True)

    steps_x = [2, 1, 3] if across == 4 else list(range(1, across))
    other_block = moved(own_block, 0, 1)
    blocks = [own_block, other_block] + [None] * (2 * across - 2)
    for dx in steps_x:
        blocks[2 * dx] = moved(own_block, dx, 0)
    for dx in steps_x:
        blocks[2 * dx + 1] = moved(other_block, dx, 0)
    source = targets // block_rows
    back = (member_index // 2 - source // 2) % across
    flip = (member_index + source) % 2
    columns = (back * 2 + flip) * block_rows + targets % block_rows
    pool_matrix, stats = pool_stage(columns, query_rows, blocks)

    hard_terms, lse, loss = hard_stage(hard_set, query_rows, stats)
    returned = lax.all_to_all(hard_terms, "group", split_axis=0, concat_axis=0, tiled=True)

    pool_weights, near, *terms = pool_back_stage(pool_matrix, columns, query_rows, lse, block_rows)
    terms = [None] + terms
    far = terms[1].astype(jnp.float32)
    arrivals = [moved(terms[2 * dx + 1], -dx, 0) for dx in steps_x]
    for arrival in arrivals:
        far = far + arrival.astype(jnp.float32)
    arrivals = [moved(terms[2 * dx], -dx, 0) for dx in steps_x]
    arrivals.append(moved(far.astype(jnp.bfloat16), 0, 1))
    grad_passages = near
    for arrival in arrivals:
        grad_passages = grad_passages + arrival.astype(jnp.float32)
    query_gradient = query_stage(hard_set, pool_matrix, query_rows, lse, pool_weights)
    grad_hard = fetch_slices(assign, returned, groups)
    return (
        loss[None],
        query_gradient[None, None],
        grad_passages[None, None],
        grad_hard[None, None],
    )


def solution(mesh):
    placed = (
        P("blk", "group", None, None),
        P("blk", "group", None, None),
        P("blk", "group", None, None),
        P("blk", "group", None),
        P(),
    )
    return jax.shard_map(
        per_device,
        mesh=mesh,
        in_specs=placed,
        out_specs=(
            P("blk", "group", None),
            P("blk", "group", None, None),
            P("blk", "group", None, None),
            P("blk", "group", None, None),
        ),
        check_vma=False,
    )
```

```python
import functools

import jax
import jax.numpy as jnp
from jax import lax
from jax.experimental import pallas as pl
from jax.experimental.pallas import tpu as pltpu
from jax.sharding import PartitionSpec as P

VMEM = pl.BlockSpec(memory_space=pltpu.VMEM)
HBM = pl.BlockSpec(memory_space=pltpu.HBM)
MIB = 1 << 20


def in_hbm(array):
    return pltpu.with_memory_space_constraint(array, pltpu.HBM)


def moved(array, dx, dy):
    count = lax.axis_size("blk")
    pairs = [(i, ((i // 2 + dx) % (count // 2)) * 2 + ((i % 2) ^ dy)) for i in range(count)]
    return lax.ppermute(array, "blk", pairs)


def exchanged(array, turn):
    groups = lax.axis_size("group")
    order = [(place - turn) % groups for place in range(groups)]
    return lax.all_to_all(
        array, "group", split_axis=0, concat_axis=0, axis_index_groups=[order], tiled=True
    )


def dot_rows(left, right):
    return lax.dot_general(
        left, right, (((1,), (1,)), ((), ())), preferred_element_type=jnp.float32
    )


def dot_plain(left, right):
    return lax.dot_general(
        left, right, (((1,), (0,)), ((), ())), preferred_element_type=jnp.float32
    )


def dot_columns(left, right):
    return lax.dot_general(
        left, right, (((0,), (0,)), ((), ())), preferred_element_type=jnp.float32
    )


def place_slices_kernel(turn, groups, slice_rows, assign_ref, hard_ref, out_ref, row, held, sem_row, sem_in, sem_out):
    own = lax.axis_index("group")
    load = pltpu.make_async_copy(assign_ref.at[own], row, sem_row)
    load.start()
    gets, puts = [], []
    for k in range(groups):
        here = pl.ds(k * slice_rows, slice_rows)
        gets.append(pltpu.make_async_copy(hard_ref.at[here], held.at[here], sem_in.at[k]))
        gets[-1].start()
    load.wait()
    for k in range(groups):
        here = pl.ds(k * slice_rows, slice_rows)
        place = lax.rem(row[k] + turn, groups)
        there = pl.ds(pl.multiple_of(place * slice_rows, slice_rows), slice_rows)
        gets[k].wait()
        puts.append(pltpu.make_async_copy(held.at[here], out_ref.at[there], sem_out.at[k]))
        puts[-1].start()
    for put in puts:
        put.wait()


def place_slices(assign, hard_rows, groups, turn):
    return pl.pallas_call(
        functools.partial(place_slices_kernel, turn, groups, hard_rows.shape[0] // groups),
        out_shape=pltpu.HBM(hard_rows.shape, hard_rows.dtype),
        in_specs=[HBM, HBM],
        out_specs=HBM,
        scratch_shapes=[
            pltpu.SMEM((groups,), jnp.int32),
            pltpu.VMEM(hard_rows.shape, hard_rows.dtype),
            pltpu.SemaphoreType.DMA,
            pltpu.SemaphoreType.DMA((groups,)),
            pltpu.SemaphoreType.DMA((groups,)),
        ],
        compiler_params=pltpu.CompilerParams(vmem_limit_bytes=4 * MIB),
        name="place_slices",
    )(in_hbm(assign), in_hbm(hard_rows))


def fetch_slices_kernel(turn, groups, slice_rows, assign_ref, back_ref, out_ref, row, held, sem_row, sem):
    own = lax.axis_index("group")
    load = pltpu.make_async_copy(assign_ref.at[own], row, sem_row)
    load.start()
    held[...] = back_ref[...].astype(jnp.float32)
    load.wait()
    puts = []
    for k in range(groups):
        here = pl.ds(k * slice_rows, slice_rows)
        place = lax.rem(row[k] + turn, groups)
        there = pl.ds(pl.multiple_of(place * slice_rows, slice_rows), slice_rows)
        puts.append(pltpu.make_async_copy(held.at[there], out_ref.at[here], sem.at[k]))
        puts[-1].start()
    for put in puts:
        put.wait()


def fetch_slices(assign, returned, groups, turn):
    return pl.pallas_call(
        functools.partial(fetch_slices_kernel, turn, groups, returned.shape[0] // groups),
        out_shape=pltpu.HBM(returned.shape, jnp.float32),
        in_specs=[HBM, VMEM],
        out_specs=HBM,
        scratch_shapes=[
            pltpu.SMEM((groups,), jnp.int32),
            pltpu.VMEM(returned.shape, jnp.float32),
            pltpu.SemaphoreType.DMA,
            pltpu.SemaphoreType.DMA((groups,)),
        ],
        compiler_params=pltpu.CompilerParams(vmem_limit_bytes=6 * MIB),
        name="fetch_slices",
    )(in_hbm(assign), returned)


def pool_kernel(part, column_ref, query_ref, *refs):
    block_refs, (pool_out, stat_out, pool, score, stat, sem) = refs[:-6], refs[-6:]
    rows = block_refs[0].shape[0]
    for c, block in enumerate(block_refs):
        pool[pl.ds(c * rows, rows), :] = block[...]
    put_pool = pltpu.make_async_copy(pool, pool_out, sem.at[0])
    put_pool.start()
    columns = column_ref[...]
    highest, picked = None, None
    steps = range(0, pool.shape[0], part)
    for start in steps:
        here = pl.ds(start, part)
        scores = dot_rows(pool[here, :], query_ref[...])
        score[here, :] = scores
        ids = start + lax.broadcasted_iota(jnp.int32, scores.shape, 0)
        peak = jnp.max(scores, axis=0, keepdims=True)
        hit = jnp.sum(jnp.where(ids == columns, scores, 0.0), axis=0, keepdims=True)
        highest = peak if highest is None else jnp.maximum(highest, peak)
        picked = hit if picked is None else picked + hit
    total = None
    for start in steps:
        some = jnp.sum(jnp.exp(score[pl.ds(start, part), :] - highest), axis=0, keepdims=True)
        total = some if total is None else total + some
    stat[0:1, :] = highest
    stat[1:2, :] = total
    stat[2:3, :] = picked
    stat[3:8, :] = jnp.zeros_like(stat[3:8, :])
    put_stat = pltpu.make_async_copy(stat, stat_out, sem.at[1])
    put_stat.start()
    put_pool.wait()
    put_stat.wait()


def pool_stage(columns, query_rows, blocks):
    rows, width = len(blocks) * blocks[0].shape[0], query_rows.shape[1]
    queries = query_rows.shape[0]
    return pl.pallas_call(
        functools.partial(pool_kernel, 512),
        out_shape=(
            pltpu.HBM((rows, width), query_rows.dtype),
            pltpu.HBM((8, queries), jnp.float32),
        ),
        in_specs=[VMEM] * (2 + len(blocks)),
        out_specs=(HBM, HBM),
        scratch_shapes=[
            pltpu.VMEM((rows, width), query_rows.dtype),
            pltpu.VMEM((rows, queries), jnp.float32),
            pltpu.VMEM((8, queries), jnp.float32),
            pltpu.SemaphoreType.DMA((2,)),
        ],
        compiler_params=pltpu.CompilerParams(vmem_limit_bytes=16 * MIB),
        cost_estimate=pl.CostEstimate(
            flops=2 * rows * queries * width, bytes_accessed=4 * MIB, transcendentals=rows * queries
        ),
        name="pool_stage",
    )(columns, query_rows, *blocks)


def hard_kernel(
    part, chunks, hard_ref, query_ref, stat_ref, term_ref, lse_ref, loss_ref, stat, score, weight, held, sem
):
    queries = query_ref.shape[0]
    load = pltpu.make_async_copy(stat_ref, stat, sem.at[0])
    load.start()
    steps = range(0, queries, part)

    def scores_of(start):
        score[:, pl.ds(start, part)] = dot_rows(hard_ref[...], query_ref[pl.ds(start, part), :])

    scores_of(0)
    load.wait()
    for start in steps:
        if start + part < queries:
            scores_of(start + part)
        here = pl.ds(start, part)
        pool_highest = stat[0:1, here]
        highest = jnp.maximum(pool_highest, jnp.max(score[:, here], axis=0, keepdims=True))
        raised = jnp.exp(score[:, here] - highest)
        total = stat[1:2, here] * jnp.exp(pool_highest - highest) + jnp.sum(
            raised, axis=0, keepdims=True
        )
        weight[:, here] = (raised * (1.0 / total)).astype(weight.dtype)
        lse = highest + jnp.log(total)
        lse_ref[:, here] = lse
        loss_ref[:, here] = lse - stat[2:3, here]
    puts, start = [], 0
    for n, chunk in enumerate(chunks):
        here = pl.ds(start, chunk)
        held[here, :] = dot_plain(weight[here, :], query_ref[...]).astype(held.dtype)
        puts.append(pltpu.make_async_copy(held.at[here], term_ref.at[here], sem.at[n + 1]))
        puts[-1].start()
        start += chunk
    for put in puts:
        put.wait()


def hard_stage(hard_set, query_rows, stats):
    rows, width = hard_set.shape
    queries = query_rows.shape[0]
    chunks = (rows // 2, rows // 4, rows // 4)
    return pl.pallas_call(
        functools.partial(hard_kernel, queries // 2, chunks),
        out_shape=(
            pltpu.HBM((rows, width), jnp.bfloat16),
            jax.ShapeDtypeStruct((1, queries), jnp.float32),
            jax.ShapeDtypeStruct((1, queries), jnp.float32),
        ),
        in_specs=[VMEM, VMEM, HBM],
        out_specs=(HBM, VMEM, VMEM),
        scratch_shapes=[
            pltpu.VMEM(stats.shape, jnp.float32),
            pltpu.VMEM((rows, queries), jnp.float32),
            pltpu.VMEM((rows, queries), jnp.bfloat16),
            pltpu.VMEM((rows, width), jnp.bfloat16),
            pltpu.SemaphoreType.DMA((1 + len(chunks),)),
        ],
        compiler_params=pltpu.CompilerParams(vmem_limit_bytes=20 * MIB),
        cost_estimate=pl.CostEstimate(
            flops=4 * rows * queries * width, bytes_accessed=8 * MIB, transcendentals=rows * queries
        ),
        name="hard_stage",
    )(hard_set, query_rows, in_hbm(stats))


def query_kernel(part, hard_ref, pool_ref, query_ref, lse_ref, pool_weight_ref, out_ref, weight, held, sem):
    queries = query_ref.shape[0]
    puts = []
    for n, start in enumerate(range(0, queries, part)):
        here = pl.ds(start, part)
        scores = dot_rows(hard_ref[...], query_ref[here, :])
        weight[:, here] = jnp.exp(scores - lse_ref[:, here]).astype(weight.dtype)
        held[here, :] = dot_columns(weight[:, here], hard_ref[...]) + dot_columns(
            pool_weight_ref[:, here], pool_ref[...]
        )
        puts.append(pltpu.make_async_copy(held.at[here], out_ref.at[here], sem.at[n]))
        puts[-1].start()
    for put in puts:
        put.wait()


def query_stage(hard_set, pool_matrix, query_rows, lse, pool_weights):
    queries, width = query_rows.shape
    rows = hard_set.shape[0]
    part = 256
    return pl.pallas_call(
        functools.partial(query_kernel, part),
        out_shape=pltpu.HBM((queries, width), jnp.float32),
        in_specs=[VMEM] * 5,
        out_specs=HBM,
        scratch_shapes=[
            pltpu.VMEM((rows, queries), jnp.bfloat16),
            pltpu.VMEM((queries, width), jnp.float32),
            pltpu.SemaphoreType.DMA((queries // part,)),
        ],
        compiler_params=pltpu.CompilerParams(vmem_limit_bytes=24 * MIB),
        cost_estimate=pl.CostEstimate(
            flops=6 * rows * queries * width, bytes_accessed=8 * MIB, transcendentals=rows * queries
        ),
        name="query_stage",
    )(hard_set, pool_matrix, query_rows, lse, pool_weights)


def pool_back_kernel(part, pool_ref, column_ref, query_ref, lse_ref, weight_ref, near_ref, *block_refs):
    rows = near_ref.shape[0]
    columns, lse = column_ref[...], lse_ref[...]
    for start in range(0, pool_ref.shape[0], part):
        here = pl.ds(start, part)
        ids = start + lax.broadcasted_iota(jnp.int32, (part, columns.shape[1]), 0)
        chance = jnp.exp(dot_rows(pool_ref[here, :], query_ref[...]) - lse)
        weight_ref[here, :] = jnp.where(ids == columns, chance - 1.0, chance).astype(weight_ref.dtype)
        terms = dot_plain(weight_ref[here, :], query_ref[...])
        for j in range(part // rows):
            piece = terms[j * rows : (j + 1) * rows]
            n = start // rows + j
            if n == 0:
                near_ref[...] = piece
            else:
                block_refs[n - 1][...] = piece.astype(block_refs[n - 1].dtype)


def pool_back_stage(pool_matrix, columns, query_rows, lse, block_rows):
    rows, width = pool_matrix.shape
    queries = query_rows.shape[0]
    others = rows // block_rows - 1
    return pl.pallas_call(
        functools.partial(pool_back_kernel, 256),
        out_shape=(
            jax.ShapeDtypeStruct((rows, queries), jnp.bfloat16),
            jax.ShapeDtypeStruct((block_rows, width), jnp.float32),
        )
        + (jax.ShapeDtypeStruct((block_rows, width), jnp.bfloat16),) * others,
        in_specs=[VMEM] * 4,
        out_specs=(VMEM,) * (2 + others),
        compiler_params=pltpu.CompilerParams(vmem_limit_bytes=24 * MIB),
        cost_estimate=pl.CostEstimate(
            flops=4 * rows * queries * width, bytes_accessed=8 * MIB, transcendentals=rows * queries
        ),
        name="pool_back_stage",
    )(pool_matrix, columns, query_rows, lse)


def per_device(queries, passages, hard_negs, positives, assign):
    query_rows = queries[0, 0]
    own_block = passages[0, 0]
    hard_rows = hard_negs[0, 0]
    targets = positives[0]
    across = lax.axis_size("blk") // 2
    groups = lax.axis_size("group")
    turn = groups // 4
    member_index = lax.axis_index("blk")
    block_rows = own_block.shape[0]

    outgoing = place_slices(assign, hard_rows, groups, turn)
    hard_set = exchanged(outgoing, turn)

    steps_x = [2, 1, 3] if across == 4 else list(range(1, across))
    other_block = moved(own_block, 0, 1)
    blocks = [own_block, other_block] + [None] * (2 * across - 2)
    for dx in steps_x:
        blocks[2 * dx] = moved(own_block, dx, 0)
    for dx in steps_x:
        blocks[2 * dx + 1] = moved(other_block, dx, 0)
    source = targets // block_rows
    back = (member_index // 2 - source // 2) % across
    flip = (member_index + source) % 2
    columns = (back * 2 + flip) * block_rows + targets % block_rows
    pool_matrix, stats = pool_stage(columns, query_rows, blocks)

    hard_terms, lse, loss = hard_stage(hard_set, query_rows, stats)
    returned = exchanged(hard_terms, turn)

    pool_weights, near, *terms = pool_back_stage(pool_matrix, columns, query_rows, lse, block_rows)
    terms = [None] + terms
    far = terms[1].astype(jnp.float32)
    arrivals = [moved(terms[2 * dx + 1], -dx, 0) for dx in steps_x]
    for arrival in arrivals:
        far = far + arrival.astype(jnp.float32)
    arrivals = [moved(terms[2 * dx], -dx, 0) for dx in steps_x]
    arrivals.append(moved(far.astype(jnp.bfloat16), 0, 1))
    grad_passages = near
    for arrival in arrivals:
        grad_passages = grad_passages + arrival.astype(jnp.float32)
    query_gradient = query_stage(hard_set, pool_matrix, query_rows, lse, pool_weights)
    grad_hard = fetch_slices(assign, returned, groups, turn)
    return (
        loss[None],
        query_gradient[None, None],
        grad_passages[None, None],
        grad_hard[None, None],
    )


def solution(mesh):
    placed = (
        P("blk", "group", None, None),
        P("blk", "group", None, None),
        P("blk", "group", None, None),
        P("blk", "group", None),
        P(),
    )
    return jax.shard_map(
        per_device,
        mesh=mesh,
        in_specs=placed,
        out_specs=(
            P("blk", "group", None),
            P("blk", "group", None, None),
            P("blk", "group", None, None),
            P("blk", "group", None, None),
        ),
        check_vma=False,
    )
```

```python
import functools

import jax
import jax.numpy as jnp
from jax import lax
from jax.experimental import pallas as pl
from jax.experimental.pallas import tpu as pltpu
from jax.sharding import PartitionSpec as P

VMEM = pl.BlockSpec(memory_space=pltpu.VMEM)
HBM = pl.BlockSpec(memory_space=pltpu.HBM)
MIB = 1 << 20


def in_hbm(array):
    return pltpu.with_memory_space_constraint(array, pltpu.HBM)


def moved(array, dx, dy):
    count = lax.axis_size("blk")
    pairs = [(i, ((i // 2 + dx) % (count // 2)) * 2 + ((i % 2) ^ dy)) for i in range(count)]
    return lax.ppermute(array, "blk", pairs)


def exchanged(array, turn):
    groups = lax.axis_size("group")
    order = [(place - turn) % groups for place in range(groups)]
    return lax.all_to_all(
        array, "group", split_axis=0, concat_axis=0, axis_index_groups=[order], tiled=True
    )


def dot_rows(left, right):
    return lax.dot_general(
        left, right, (((1,), (1,)), ((), ())), preferred_element_type=jnp.float32
    )


def dot_plain(left, right):
    return lax.dot_general(
        left, right, (((1,), (0,)), ((), ())), preferred_element_type=jnp.float32
    )


def dot_columns(left, right):
    return lax.dot_general(
        left, right, (((0,), (0,)), ((), ())), preferred_element_type=jnp.float32
    )


def place_slices_kernel(turn, groups, slice_rows, assign_ref, hard_ref, out_ref, row, held, sem_row, sem_in, sem_out):
    own = lax.axis_index("group")
    load = pltpu.make_async_copy(assign_ref.at[own], row, sem_row)
    load.start()
    gets, puts = [], []
    for k in range(groups):
        here = pl.ds(k * slice_rows, slice_rows)
        gets.append(pltpu.make_async_copy(hard_ref.at[here], held.at[here], sem_in.at[k]))
        gets[-1].start()
    load.wait()
    for k in range(groups):
        here = pl.ds(k * slice_rows, slice_rows)
        place = lax.rem(row[k] + turn, groups)
        there = pl.ds(pl.multiple_of(place * slice_rows, slice_rows), slice_rows)
        gets[k].wait()
        puts.append(pltpu.make_async_copy(held.at[here], out_ref.at[there], sem_out.at[k]))
        puts[-1].start()
    for put in puts:
        put.wait()


def place_slices(assign, hard_rows, groups, turn):
    return pl.pallas_call(
        functools.partial(place_slices_kernel, turn, groups, hard_rows.shape[0] // groups),
        out_shape=pltpu.HBM(hard_rows.shape, hard_rows.dtype),
        in_specs=[HBM, HBM],
        out_specs=HBM,
        scratch_shapes=[
            pltpu.SMEM((groups,), jnp.int32),
            pltpu.VMEM(hard_rows.shape, hard_rows.dtype),
            pltpu.SemaphoreType.DMA,
            pltpu.SemaphoreType.DMA((groups,)),
            pltpu.SemaphoreType.DMA((groups,)),
        ],
        compiler_params=pltpu.CompilerParams(vmem_limit_bytes=4 * MIB),
        name="place_slices",
    )(in_hbm(assign), in_hbm(hard_rows))


def fetch_slices_kernel(turn, groups, slice_rows, assign_ref, back_ref, out_ref, row, held, sem_row, sem):
    own = lax.axis_index("group")
    load = pltpu.make_async_copy(assign_ref.at[own], row, sem_row)
    load.start()
    held[...] = back_ref[...].astype(jnp.float32)
    load.wait()
    puts = []
    for k in range(groups):
        here = pl.ds(k * slice_rows, slice_rows)
        place = lax.rem(row[k] + turn, groups)
        there = pl.ds(pl.multiple_of(place * slice_rows, slice_rows), slice_rows)
        puts.append(pltpu.make_async_copy(held.at[there], out_ref.at[here], sem.at[k]))
        puts[-1].start()
    for put in puts:
        put.wait()


def fetch_slices(assign, returned, groups, turn):
    return pl.pallas_call(
        functools.partial(fetch_slices_kernel, turn, groups, returned.shape[0] // groups),
        out_shape=pltpu.HBM(returned.shape, jnp.float32),
        in_specs=[VMEM, VMEM],
        out_specs=HBM,
        scratch_shapes=[
            pltpu.SMEM((groups,), jnp.int32),
            pltpu.VMEM(returned.shape, jnp.float32),
            pltpu.SemaphoreType.DMA,
            pltpu.SemaphoreType.DMA((groups,)),
        ],
        compiler_params=pltpu.CompilerParams(vmem_limit_bytes=6 * MIB),
        name="fetch_slices",
    )(assign, returned)


def pool_kernel(part, column_ref, query_ref, *refs):
    block_refs, (near_out, far_out, stat_out, pool, score, stat, sem) = refs[:-7], refs[-7:]
    rows = block_refs[0].shape[0]
    half = near_out.shape[0]
    for c, block in enumerate(block_refs):
        pool[pl.ds(c * rows, rows), :] = block[...]
    puts = [
        pltpu.make_async_copy(pool.at[pl.ds(0, half)], near_out, sem.at[0]),
        pltpu.make_async_copy(pool.at[pl.ds(half, half)], far_out, sem.at[1]),
        pltpu.make_async_copy(stat, stat_out, sem.at[2]),
    ]
    puts[0].start()
    puts[1].start()
    columns = column_ref[...]
    highest, picked = None, None
    steps = range(0, pool.shape[0], part)
    for start in steps:
        here = pl.ds(start, part)
        scores = dot_rows(pool[here, :], query_ref[...])
        score[here, :] = scores
        ids = start + lax.broadcasted_iota(jnp.int32, scores.shape, 0)
        peak = jnp.max(scores, axis=0, keepdims=True)
        hit = jnp.sum(jnp.where(ids == columns, scores, 0.0), axis=0, keepdims=True)
        highest = peak if highest is None else jnp.maximum(highest, peak)
        picked = hit if picked is None else picked + hit
    total = None
    for start in steps:
        some = jnp.sum(jnp.exp(score[pl.ds(start, part), :] - highest), axis=0, keepdims=True)
        total = some if total is None else total + some
    stat[0:1, :] = highest
    stat[1:2, :] = total
    stat[2:3, :] = picked
    stat[3:8, :] = jnp.zeros_like(stat[3:8, :])
    puts[2].start()
    for put in puts:
        put.wait()


def pool_stage(columns, query_rows, blocks):
    rows, width = len(blocks) * blocks[0].shape[0], query_rows.shape[1]
    queries = query_rows.shape[0]
    return pl.pallas_call(
        functools.partial(pool_kernel, 512),
        out_shape=(
            pltpu.HBM((rows // 2, width), query_rows.dtype),
            pltpu.HBM((rows // 2, width), query_rows.dtype),
            pltpu.HBM((8, queries), jnp.float32),
        ),
        in_specs=[VMEM] * (2 + len(blocks)),
        out_specs=(HBM, HBM, HBM),
        scratch_shapes=[
            pltpu.VMEM((rows, width), query_rows.dtype),
            pltpu.VMEM((rows, queries), jnp.float32),
            pltpu.VMEM((8, queries), jnp.float32),
            pltpu.SemaphoreType.DMA((3,)),
        ],
        compiler_params=pltpu.CompilerParams(vmem_limit_bytes=16 * MIB),
        cost_estimate=pl.CostEstimate(
            flops=2 * rows * queries * width, bytes_accessed=4 * MIB, transcendentals=rows * queries
        ),
        name="pool_stage",
    )(columns, query_rows, *blocks)


def hard_kernel(
    part, chunks, hard_ref, query_ref, stat_ref, term_ref, lse_ref, loss_ref, stat, score, weight, held, sem
):
    queries = query_ref.shape[0]
    load = pltpu.make_async_copy(stat_ref, stat, sem.at[0])
    load.start()
    steps = range(0, queries, part)

    def scores_of(start):
        score[:, pl.ds(start, part)] = dot_rows(hard_ref[...], query_ref[pl.ds(start, part), :])

    scores_of(0)
    load.wait()
    for start in steps:
        if start + part < queries:
            scores_of(start + part)
        here = pl.ds(start, part)
        pool_highest = stat[0:1, here]
        highest = jnp.maximum(pool_highest, jnp.max(score[:, here], axis=0, keepdims=True))
        raised = jnp.exp(score[:, here] - highest)
        total = stat[1:2, here] * jnp.exp(pool_highest - highest) + jnp.sum(
            raised, axis=0, keepdims=True
        )
        weight[:, here] = (raised * (1.0 / total)).astype(weight.dtype)
        lse = highest + jnp.log(total)
        lse_ref[:, here] = lse
        loss_ref[:, here] = lse - stat[2:3, here]
    puts, start = [], 0
    for n, chunk in enumerate(chunks):
        here = pl.ds(start, chunk)
        held[here, :] = dot_plain(weight[here, :], query_ref[...]).astype(held.dtype)
        puts.append(pltpu.make_async_copy(held.at[here], term_ref.at[here], sem.at[n + 1]))
        puts[-1].start()
        start += chunk
    for put in puts:
        put.wait()


def hard_stage(hard_set, query_rows, stats):
    rows, width = hard_set.shape
    queries = query_rows.shape[0]
    chunks = (rows // 2, rows // 4, rows // 4)
    return pl.pallas_call(
        functools.partial(hard_kernel, queries // 2, chunks),
        out_shape=(
            pltpu.HBM((rows, width), jnp.bfloat16),
            jax.ShapeDtypeStruct((1, queries), jnp.float32),
            jax.ShapeDtypeStruct((1, queries), jnp.float32),
        ),
        in_specs=[VMEM, VMEM, HBM],
        out_specs=(HBM, VMEM, VMEM),
        scratch_shapes=[
            pltpu.VMEM(stats.shape, jnp.float32),
            pltpu.VMEM((rows, queries), jnp.float32),
            pltpu.VMEM((rows, queries), jnp.bfloat16),
            pltpu.VMEM((rows, width), jnp.bfloat16),
            pltpu.SemaphoreType.DMA((1 + len(chunks),)),
        ],
        compiler_params=pltpu.CompilerParams(vmem_limit_bytes=20 * MIB),
        cost_estimate=pl.CostEstimate(
            flops=4 * rows * queries * width, bytes_accessed=8 * MIB, transcendentals=rows * queries
        ),
        name="hard_stage",
    )(hard_set, query_rows, in_hbm(stats))


def query_kernel(
    part, hard_ref, near_ref, far_ref, query_ref, lse_ref, near_weight, far_weight, out_ref, weight, held, sem
):
    queries = query_ref.shape[0]
    puts = []
    for n, start in enumerate(range(0, queries, part)):
        here = pl.ds(start, part)
        scores = dot_rows(hard_ref[...], query_ref[here, :])
        weight[:, here] = jnp.exp(scores - lse_ref[:, here]).astype(weight.dtype)
        held[here, :] = (
            dot_columns(weight[:, here], hard_ref[...])
            + dot_columns(near_weight[:, here], near_ref[...])
            + dot_columns(far_weight[:, here], far_ref[...])
        )
        puts.append(pltpu.make_async_copy(held.at[here], out_ref.at[here], sem.at[n]))
        puts[-1].start()
    for put in puts:
        put.wait()


def query_stage(hard_set, near_pool, far_pool, query_rows, lse, near_weights, far_weights):
    queries, width = query_rows.shape
    rows = hard_set.shape[0]
    part = 256
    return pl.pallas_call(
        functools.partial(query_kernel, part),
        out_shape=pltpu.HBM((queries, width), jnp.float32),
        in_specs=[VMEM] * 7,
        out_specs=HBM,
        scratch_shapes=[
            pltpu.VMEM((rows, queries), jnp.bfloat16),
            pltpu.VMEM((queries, width), jnp.float32),
            pltpu.SemaphoreType.DMA((queries // part,)),
        ],
        compiler_params=pltpu.CompilerParams(vmem_limit_bytes=24 * MIB),
        cost_estimate=pl.CostEstimate(
            flops=6 * rows * queries * width, bytes_accessed=8 * MIB, transcendentals=rows * queries
        ),
        name="query_stage",
    )(hard_set, near_pool, far_pool, query_rows, lse, near_weights, far_weights)


def pool_back_kernel(part, first, pool_ref, column_ref, query_ref, lse_ref, weight_ref, own_ref, *block_refs):
    rows = own_ref.shape[0]
    columns, lse = column_ref[...], lse_ref[...]
    for start in range(0, pool_ref.shape[0], part):
        here = pl.ds(start, part)
        ids = first + start + lax.broadcasted_iota(jnp.int32, (part, columns.shape[1]), 0)
        chance = jnp.exp(dot_rows(pool_ref[here, :], query_ref[...]) - lse)
        weight_ref[here, :] = jnp.where(ids == columns, chance - 1.0, chance).astype(weight_ref.dtype)
        terms = dot_plain(weight_ref[here, :], query_ref[...])
        for j in range(part // rows):
            piece = terms[j * rows : (j + 1) * rows]
            n = start // rows + j
            if n == 0:
                own_ref[...] = piece
            else:
                block_refs[n - 1][...] = piece.astype(block_refs[n - 1].dtype)


def pool_back_stage(pool_half, first, columns, query_rows, lse, block_rows):
    rows, width = pool_half.shape
    queries = query_rows.shape[0]
    others = rows // block_rows - 1
    return pl.pallas_call(
        functools.partial(pool_back_kernel, 256, first),
        out_shape=(
            jax.ShapeDtypeStruct((rows, queries), jnp.bfloat16),
            jax.ShapeDtypeStruct((block_rows, width), jnp.float32),
        )
        + (jax.ShapeDtypeStruct((block_rows, width), jnp.bfloat16),) * others,
        in_specs=[VMEM] * 4,
        out_specs=(VMEM,) * (2 + others),
        compiler_params=pltpu.CompilerParams(vmem_limit_bytes=20 * MIB),
        cost_estimate=pl.CostEstimate(
            flops=4 * rows * queries * width, bytes_accessed=4 * MIB, transcendentals=rows * queries
        ),
        name="pool_back_stage",
    )(pool_half, columns, query_rows, lse)


def per_device(queries, passages, hard_negs, positives, assign):
    query_rows = queries[0, 0]
    own_block = passages[0, 0]
    hard_rows = hard_negs[0, 0]
    targets = positives[0]
    across = lax.axis_size("blk") // 2
    groups = lax.axis_size("group")
    turn = groups // 4
    member_index = lax.axis_index("blk")
    block_rows = own_block.shape[0]

    outgoing = place_slices(assign, hard_rows, groups, turn)
    hard_set = exchanged(outgoing, turn)

    steps_x = [2, 1, 3] if across == 4 else list(range(1, across))
    other_block = moved(own_block, 0, 1)
    blocks = [None] * (2 * across)
    blocks[0], blocks[across] = own_block, other_block
    for dx in steps_x:
        blocks[dx] = moved(own_block, dx, 0)
    for dx in steps_x:
        blocks[across + dx] = moved(other_block, dx, 0)
    source = targets // block_rows
    back = (member_index // 2 - source // 2) % across
    flip = (member_index + source) % 2
    columns = (flip * across + back) * block_rows + targets % block_rows
    near_pool, far_pool, stats = pool_stage(columns, query_rows, blocks)

    hard_terms, lse, loss = hard_stage(hard_set, query_rows, stats)
    returned = exchanged(hard_terms, turn)

    far_weights, far, *far_terms = pool_back_stage(
        far_pool, across * block_rows, columns, query_rows, lse, block_rows
    )
    arrivals = [moved(far_terms[dx - 1], -dx, 0) for dx in steps_x]
    for arrival in arrivals:
        far = far + arrival.astype(jnp.float32)
    near_weights, near, *near_terms = pool_back_stage(
        near_pool, 0, columns, query_rows, lse, block_rows
    )
    arrivals = [moved(near_terms[dx - 1], -dx, 0) for dx in steps_x]
    arrivals.append(moved(far.astype(jnp.bfloat16), 0, 1))
    grad_passages = near
    for arrival in arrivals:
        grad_passages = grad_passages + arrival.astype(jnp.float32)
    query_gradient = query_stage(
        hard_set, near_pool, far_pool, query_rows, lse, near_weights, far_weights
    )
    grad_hard = fetch_slices(assign, returned, groups, turn)
    return (
        loss[None],
        query_gradient[None, None],
        grad_passages[None, None],
        grad_hard[None, None],
    )


def solution(mesh):
    placed = (
        P("blk", "group", None, None),
        P("blk", "group", None, None),
        P("blk", "group", None, None),
        P("blk", "group", None),
        P(),
    )
    return jax.shard_map(
        per_device,
        mesh=mesh,
        in_specs=placed,
        out_specs=(
            P("blk", "group", None),
            P("blk", "group", None, None),
            P("blk", "group", None, None),
            P("blk", "group", None, None),
        ),
        check_vma=False,
    )
```

```python
import functools

import jax
import jax.numpy as jnp
from jax import lax
from jax.experimental import pallas as pl
from jax.experimental.pallas import tpu as pltpu
from jax.sharding import PartitionSpec as P

VMEM = pl.BlockSpec(memory_space=pltpu.VMEM)
HBM = pl.BlockSpec(memory_space=pltpu.HBM)
MIB = 1 << 20


def in_hbm(array):
    return pltpu.with_memory_space_constraint(array, pltpu.HBM)


def moved(array, dx, dy):
    count = lax.axis_size("blk")
    pairs = [(i, ((i // 2 + dx) % (count // 2)) * 2 + ((i % 2) ^ dy)) for i in range(count)]
    return lax.ppermute(array, "blk", pairs)


def exchanged(array, turn):
    groups = lax.axis_size("group")
    order = [(place - turn) % groups for place in range(groups)]
    return lax.all_to_all(
        array, "group", split_axis=0, concat_axis=0, axis_index_groups=[order], tiled=True
    )


def dot_rows(left, right):
    return lax.dot_general(
        left, right, (((1,), (1,)), ((), ())), preferred_element_type=jnp.float32
    )


def dot_plain(left, right):
    return lax.dot_general(
        left, right, (((1,), (0,)), ((), ())), preferred_element_type=jnp.float32
    )


def dot_columns(left, right):
    return lax.dot_general(
        left, right, (((0,), (0,)), ((), ())), preferred_element_type=jnp.float32
    )


def place_slices_kernel(turn, groups, slice_rows, assign_ref, hard_ref, out_ref, row, held, sem_row, sem_in, sem_out):
    own = lax.axis_index("group")
    load = pltpu.make_async_copy(assign_ref.at[own], row, sem_row)
    load.start()
    gets, puts = [], []
    for k in range(groups):
        here = pl.ds(k * slice_rows, slice_rows)
        gets.append(pltpu.make_async_copy(hard_ref.at[here], held.at[here], sem_in.at[k]))
        gets[-1].start()
    load.wait()
    for k in range(groups):
        here = pl.ds(k * slice_rows, slice_rows)
        place = lax.rem(row[k] + turn, groups)
        there = pl.ds(pl.multiple_of(place * slice_rows, slice_rows), slice_rows)
        gets[k].wait()
        puts.append(pltpu.make_async_copy(held.at[here], out_ref.at[there], sem_out.at[k]))
        puts[-1].start()
    for put in puts:
        put.wait()


def place_slices(assign, hard_rows, groups, turn):
    return pl.pallas_call(
        functools.partial(place_slices_kernel, turn, groups, hard_rows.shape[0] // groups),
        out_shape=pltpu.HBM(hard_rows.shape, hard_rows.dtype),
        in_specs=[HBM, HBM],
        out_specs=HBM,
        scratch_shapes=[
            pltpu.SMEM((groups,), jnp.int32),
            pltpu.VMEM(hard_rows.shape, hard_rows.dtype),
            pltpu.SemaphoreType.DMA,
            pltpu.SemaphoreType.DMA((groups,)),
            pltpu.SemaphoreType.DMA((groups,)),
        ],
        compiler_params=pltpu.CompilerParams(vmem_limit_bytes=4 * MIB),
        name="place_slices",
    )(in_hbm(assign), in_hbm(hard_rows))


def fetch_slices_kernel(turn, groups, slice_rows, assign_ref, back_ref, out_ref, row, held, sem_row, sem):
    own = lax.axis_index("group")
    load = pltpu.make_async_copy(assign_ref.at[own], row, sem_row)
    load.start()
    held[...] = back_ref[...].astype(jnp.float32)
    load.wait()
    puts = []
    for k in range(groups):
        here = pl.ds(k * slice_rows, slice_rows)
        place = lax.rem(row[k] + turn, groups)
        there = pl.ds(pl.multiple_of(place * slice_rows, slice_rows), slice_rows)
        puts.append(pltpu.make_async_copy(held.at[there], out_ref.at[here], sem.at[k]))
        puts[-1].start()
    for put in puts:
        put.wait()


def fetch_slices(assign, returned, groups, turn):
    return pl.pallas_call(
        functools.partial(fetch_slices_kernel, turn, groups, returned.shape[0] // groups),
        out_shape=pltpu.HBM(returned.shape, jnp.float32),
        in_specs=[VMEM, VMEM],
        out_specs=HBM,
        scratch_shapes=[
            pltpu.SMEM((groups,), jnp.int32),
            pltpu.VMEM(returned.shape, jnp.float32),
            pltpu.SemaphoreType.DMA,
            pltpu.SemaphoreType.DMA((groups,)),
        ],
        compiler_params=pltpu.CompilerParams(vmem_limit_bytes=6 * MIB),
        name="fetch_slices",
    )(assign, returned)


def pool_kernel(part, column_ref, query_ref, *refs):
    block_refs, (pool_out, stat_out, pool, score, stat, sem) = refs[:-6], refs[-6:]
    rows = block_refs[0].shape[0]
    for c, block in enumerate(block_refs):
        pool[pl.ds(c * rows, rows), :] = block[...]
    put_pool = pltpu.make_async_copy(pool, pool_out, sem.at[0])
    put_pool.start()
    columns = column_ref[...]
    highest, picked = None, None
    steps = range(0, pool.shape[0], part)
    for start in steps:
        here = pl.ds(start, part)
        scores = dot_rows(pool[here, :], query_ref[...])
        score[here, :] = scores
        ids = start + lax.broadcasted_iota(jnp.int32, scores.shape, 0)
        peak = jnp.max(scores, axis=0, keepdims=True)
        hit = jnp.sum(jnp.where(ids == columns, scores, 0.0), axis=0, keepdims=True)
        highest = peak if highest is None else jnp.maximum(highest, peak)
        picked = hit if picked is None else picked + hit
    total = None
    for start in steps:
        some = jnp.sum(jnp.exp(score[pl.ds(start, part), :] - highest), axis=0, keepdims=True)
        total = some if total is None else total + some
    stat[0:1, :] = highest
    stat[1:2, :] = total
    stat[2:3, :] = picked
    stat[3:8, :] = jnp.zeros_like(stat[3:8, :])
    put_stat = pltpu.make_async_copy(stat, stat_out, sem.at[1])
    put_stat.start()
    put_pool.wait()
    put_stat.wait()


def pool_stage(columns, query_rows, blocks):
    rows, width = len(blocks) * blocks[0].shape[0], query_rows.shape[1]
    queries = query_rows.shape[0]
    return pl.pallas_call(
        functools.partial(pool_kernel, 512),
        out_shape=(
            pltpu.HBM((rows, width), query_rows.dtype),
            pltpu.HBM((8, queries), jnp.float32),
        ),
        in_specs=[VMEM] * (2 + len(blocks)),
        out_specs=(HBM, HBM),
        scratch_shapes=[
            pltpu.VMEM((rows, width), query_rows.dtype),
            pltpu.VMEM((rows, queries), jnp.float32),
            pltpu.VMEM((8, queries), jnp.float32),
            pltpu.SemaphoreType.DMA((2,)),
        ],
        compiler_params=pltpu.CompilerParams(vmem_limit_bytes=16 * MIB),
        cost_estimate=pl.CostEstimate(
            flops=2 * rows * queries * width, bytes_accessed=4 * MIB, transcendentals=rows * queries
        ),
        name="pool_stage",
    )(columns, query_rows, *blocks)


def hard_kernel(
    part, chunks, hard_ref, query_ref, stat_ref, term_ref, lse_ref, loss_ref, stat, score, weight, held, sem
):
    queries = query_ref.shape[0]
    load = pltpu.make_async_copy(stat_ref, stat, sem.at[0])
    load.start()
    steps = range(0, queries, part)

    def scores_of(start):
        score[:, pl.ds(start, part)] = dot_rows(hard_ref[...], query_ref[pl.ds(start, part), :])

    scores_of(0)
    load.wait()
    for start in steps:
        if start + part < queries:
            scores_of(start + part)
        here = pl.ds(start, part)
        pool_highest = stat[0:1, here]
        highest = jnp.maximum(pool_highest, jnp.max(score[:, here], axis=0, keepdims=True))
        raised = jnp.exp(score[:, here] - highest)
        total = stat[1:2, here] * jnp.exp(pool_highest - highest) + jnp.sum(
            raised, axis=0, keepdims=True
        )
        weight[:, here] = (raised * (1.0 / total)).astype(weight.dtype)
        lse = highest + jnp.log(total)
        lse_ref[:, here] = lse
        loss_ref[:, here] = lse - stat[2:3, here]
    puts, start = [], 0
    for n, chunk in enumerate(chunks):
        here = pl.ds(start, chunk)
        held[here, :] = dot_plain(weight[here, :], query_ref[...]).astype(held.dtype)
        puts.append(pltpu.make_async_copy(held.at[here], term_ref.at[here], sem.at[n + 1]))
        puts[-1].start()
        start += chunk
    for put in puts:
        put.wait()


def hard_stage(hard_set, query_rows, stats):
    rows, width = hard_set.shape
    queries = query_rows.shape[0]
    chunks = (rows // 2, rows // 4, rows // 4)
    return pl.pallas_call(
        functools.partial(hard_kernel, queries // 2, chunks),
        out_shape=(
            pltpu.HBM((rows, width), jnp.bfloat16),
            jax.ShapeDtypeStruct((1, queries), jnp.float32),
            jax.ShapeDtypeStruct((1, queries), jnp.float32),
        ),
        in_specs=[VMEM, VMEM, HBM],
        out_specs=(HBM, VMEM, VMEM),
        scratch_shapes=[
            pltpu.VMEM(stats.shape, jnp.float32),
            pltpu.VMEM((rows, queries), jnp.float32),
            pltpu.VMEM((rows, queries), jnp.bfloat16),
            pltpu.VMEM((rows, width), jnp.bfloat16),
            pltpu.SemaphoreType.DMA((1 + len(chunks),)),
        ],
        compiler_params=pltpu.CompilerParams(vmem_limit_bytes=20 * MIB),
        cost_estimate=pl.CostEstimate(
            flops=4 * rows * queries * width, bytes_accessed=8 * MIB, transcendentals=rows * queries
        ),
        name="hard_stage",
    )(hard_set, query_rows, in_hbm(stats))


def query_kernel(part, hard_ref, pool_ref, query_ref, lse_ref, pool_weight_ref, out_ref, weight, held, sem):
    queries = query_ref.shape[0]
    puts = []
    for n, start in enumerate(range(0, queries, part)):
        here = pl.ds(start, part)
        scores = dot_rows(hard_ref[...], query_ref[here, :])
        weight[:, here] = jnp.exp(scores - lse_ref[:, here]).astype(weight.dtype)
        held[here, :] = dot_columns(weight[:, here], hard_ref[...]) + dot_columns(
            pool_weight_ref[:, here], pool_ref[...]
        )
        puts.append(pltpu.make_async_copy(held.at[here], out_ref.at[here], sem.at[n]))
        puts[-1].start()
    for put in puts:
        put.wait()


def query_stage(hard_set, pool_matrix, query_rows, lse, pool_weights):
    queries, width = query_rows.shape
    rows = hard_set.shape[0]
    part = 256
    return pl.pallas_call(
        functools.partial(query_kernel, part),
        out_shape=pltpu.HBM((queries, width), jnp.float32),
        in_specs=[VMEM] * 5,
        out_specs=HBM,
        scratch_shapes=[
            pltpu.VMEM((rows, queries), jnp.bfloat16),
            pltpu.VMEM((queries, width), jnp.float32),
            pltpu.SemaphoreType.DMA((queries // part,)),
        ],
        compiler_params=pltpu.CompilerParams(vmem_limit_bytes=24 * MIB),
        cost_estimate=pl.CostEstimate(
            flops=6 * rows * queries * width, bytes_accessed=8 * MIB, transcendentals=rows * queries
        ),
        name="query_stage",
    )(hard_set, pool_matrix, query_rows, lse, pool_weights)


def pool_back_kernel(part, pool_ref, column_ref, query_ref, lse_ref, weight_ref, near_ref, *block_refs):
    rows = near_ref.shape[0]
    columns, lse = column_ref[...], lse_ref[...]
    for start in range(0, pool_ref.shape[0], part):
        here = pl.ds(start, part)
        ids = start + lax.broadcasted_iota(jnp.int32, (part, columns.shape[1]), 0)
        chance = jnp.exp(dot_rows(pool_ref[here, :], query_ref[...]) - lse)
        weight_ref[here, :] = jnp.where(ids == columns, chance - 1.0, chance).astype(weight_ref.dtype)
        terms = dot_plain(weight_ref[here, :], query_ref[...])
        for j in range(part // rows):
            piece = terms[j * rows : (j + 1) * rows]
            n = start // rows + j
            if n == 0:
                near_ref[...] = piece
            else:
                block_refs[n - 1][...] = piece.astype(block_refs[n - 1].dtype)


def pool_back_stage(pool_matrix, columns, query_rows, lse, block_rows):
    rows, width = pool_matrix.shape
    queries = query_rows.shape[0]
    others = rows // block_rows - 1
    return pl.pallas_call(
        functools.partial(pool_back_kernel, 256),
        out_shape=(
            jax.ShapeDtypeStruct((rows, queries), jnp.bfloat16),
            jax.ShapeDtypeStruct((block_rows, width), jnp.float32),
        )
        + (jax.ShapeDtypeStruct((block_rows, width), jnp.bfloat16),) * others,
        in_specs=[VMEM] * 4,
        out_specs=(VMEM,) * (2 + others),
        compiler_params=pltpu.CompilerParams(vmem_limit_bytes=24 * MIB),
        cost_estimate=pl.CostEstimate(
            flops=4 * rows * queries * width, bytes_accessed=8 * MIB, transcendentals=rows * queries
        ),
        name="pool_back_stage",
    )(pool_matrix, columns, query_rows, lse)


def per_device(queries, passages, hard_negs, positives, assign):
    query_rows = queries[0, 0]
    own_block = passages[0, 0]
    hard_rows = hard_negs[0, 0]
    targets = positives[0]
    across = lax.axis_size("blk") // 2
    groups = lax.axis_size("group")
    turn = groups // 4
    member_index = lax.axis_index("blk")
    block_rows = own_block.shape[0]

    outgoing = place_slices(assign, hard_rows, groups, turn)
    hard_set = exchanged(outgoing, turn)

    steps_x = [2, 1, 3] if across == 4 else list(range(1, across))
    other_block = moved(own_block, 0, 1)
    blocks = [own_block, other_block] + [None] * (2 * across - 2)
    for dx in steps_x:
        blocks[2 * dx] = moved(own_block, dx, 0)
    for dx in steps_x:
        blocks[2 * dx + 1] = moved(other_block, dx, 0)
    source = targets // block_rows
    back = (member_index // 2 - source // 2) % across
    flip = (member_index + source) % 2
    columns = (back * 2 + flip) * block_rows + targets % block_rows
    pool_matrix, stats = pool_stage(columns, query_rows, blocks)

    hard_terms, lse, loss = hard_stage(hard_set, query_rows, stats)
    returned = exchanged(hard_terms, turn)

    pool_weights, near, *terms = pool_back_stage(pool_matrix, columns, query_rows, lse, block_rows)
    terms = [None] + terms
    far = terms[1].astype(jnp.float32)
    arrivals = [moved(terms[2 * dx + 1], -dx, 0) for dx in steps_x]
    for arrival in arrivals:
        far = far + arrival.astype(jnp.float32)
    arrivals = [moved(terms[2 * dx], -dx, 0) for dx in steps_x]
    arrivals.append(moved(far.astype(jnp.bfloat16), 0, 1))
    grad_passages = near
    for arrival in arrivals:
        grad_passages = grad_passages + arrival.astype(jnp.float32)
    query_gradient = query_stage(hard_set, pool_matrix, query_rows, lse, pool_weights)
    grad_hard = fetch_slices(assign, returned, groups, turn)
    return (
        loss[None],
        query_gradient[None, None],
        grad_passages[None, None],
        grad_hard[None, None],
    )


def solution(mesh):
    placed = (
        P("blk", "group", None, None),
        P("blk", "group", None, None),
        P("blk", "group", None, None),
        P("blk", "group", None),
        P(),
    )
    return jax.shard_map(
        per_device,
        mesh=mesh,
        in_specs=placed,
        out_specs=(
            P("blk", "group", None),
            P("blk", "group", None, None),
            P("blk", "group", None, None),
            P("blk", "group", None, None),
        ),
        check_vma=False,
    )
```
